32 devices in a mesh: tm: 8 (over z, x), space: 4 (over y, core).
Axes of the slice: x: 2, y: 2, z: 4, core: 2. Of those that a mesh axis runs over, the one named last changes fastest.
Arguments:
- forcing: float32 [8, 16, 32, 1024], P('tm', 'space'), may hold values from -6 to 6
- inv_density: bfloat16 [8, 16, 32, 1024], P('tm', 'space'), may hold values from 0.049804688 to 0.5
- wall_mask: int32 [16, 32, 1024], P('space'), may hold values 0 or 1
- guess: float32 [8, 16, 32, 1024], P('tm', 'space'), may hold values from -4 to 4
Outputs:
- pressure: float32 [8, 16, 32, 1024], P('tm', 'space')
- residual: float32 [8, 16, 32, 1024], P('tm', 'space')
The draws below stay inside these ranges and needn't reach their ends.
All inputs are finite; a program needn't handle non-finite values. No bound on the sum of `wall_mask` on one device may be relied on, other than what follows from the above.
Results may differ from the reference program's by a relative error of at most 0.0003.
Values sent between devices are 32-bit elements; how exact they have to be, the bound alone decides.
A program may use at most 64 MiB of HBM per device.

```python
import math
import jax
import jax.numpy as jnp

CELLS_X = 32
CELLS_Y = 1024
STEPS_DEV = 1
SWEEPS = 2
ITERS = 2
STEPS = 8
PLANES = 16
N_TM = 8


def set_ends(array, key, least, high):
    longest = array.shape.index(max(array.shape))
    spots = []
    for shift in (0, 1):
        where = [jax.random.randint(jax.random.fold_in(key, axis), (), 0, length) for axis, length in enumerate(array.shape)]
        where[longest] = (where[longest] + shift) % array.shape[longest]
        spots.append(tuple(where))
    return array.at[spots[0]].set(least).at[spots[1]].set(high)


def block_levels(rng, dims, split, least, top_value):
    loudness, own = 1.0, jax.random.fold_in(rng, 6)
    for axis_at, parts in split:
        heights = jnp.exp(jax.random.uniform(jax.random.fold_in(own, axis_at), (parts,), jnp.float32, least / len(split), top_value / len(split)))
        loudness = loudness * jnp.repeat(heights, dims[axis_at] // parts).reshape([-1 if axis == axis_at else 1 for axis in range(len(dims))])
    return loudness


def gaussian(stream_key, extent, deviation, bound, shards=(), dtype=jnp.bfloat16):
    drawn = deviation * jax.random.normal(stream_key, extent, jnp.float32)
    if shards:
        drawn = drawn * block_levels(stream_key, extent, shards, -0.22, 0.18)
    return jnp.clip(drawn, -bound, bound).astype(dtype)


def setup_inputs(seed: int = 0) -> dict:
    splits = jax.random.split(jax.random.key(seed), 5)
    forcing = gaussian(splits[0], (STEPS, PLANES, CELLS_X, CELLS_Y), 1.0, 6.0, ((0, 8), (1, 4)), jnp.float32)
    inv_density = jnp.clip(jnp.exp(math.log(0.5) - 2.306499 * jax.random.uniform(splits[1], (STEPS, PLANES, CELLS_X, CELLS_Y), jnp.float32) ** block_levels(splits[1], (STEPS, PLANES, CELLS_X, CELLS_Y), ((0, 8), (1, 4)), -0.2, 0.2)), 0.049804688, 0.5).astype(jnp.bfloat16)
    wall_mask = set_ends((jax.random.randint(splits[2], (PLANES, CELLS_X, CELLS_Y), 0, 8) < 7).astype(jnp.int32), jax.random.fold_in(splits[2], 1), 0, 1)
    guess = gaussian(splits[3], (STEPS, PLANES, CELLS_X, CELLS_Y), 0.3, 4.0, ((0, 8), (1, 4)), jnp.float32)
    return dict(forcing=forcing, inv_density=inv_density, wall_mask=wall_mask, guess=guess)


def neighbours(field):
    lead = [(0, 0)] * (field.ndim - 3)
    padded = jnp.pad(field, lead + [(1, 1), (1, 1), (1, 1)])
    beside = padded[..., 2:, 1:-1, 1:-1] + padded[..., :-2, 1:-1, 1:-1]
    beside = beside + padded[..., 1:-1, 2:, 1:-1] + padded[..., 1:-1, :-2, 1:-1]
    beside = beside + padded[..., 1:-1, 1:-1, 2:] + padded[..., 1:-1, 1:-1, :-2]
    return beside


def reference(forcing, inv_density, wall_mask, guess):
    shape = (N_TM, STEPS_DEV) + forcing.shape[1:]
    force_slab = forcing.reshape(shape)
    dens_slab = inv_density.astype(jnp.float32).reshape(shape)
    mask_float = wall_mask.astype(jnp.float32)
    pressure = guess
    for it in range(ITERS):
        old = pressure
        old_slab = old.reshape(shape)
        rolled_one = jnp.roll(old, 1, axis=0).reshape(shape)
        rolled_two = jnp.roll(old, 2, axis=0).reshape(shape)
        fresh = []
        for step in range(STEPS_DEV):
            if step >= 1:
                last_state = fresh[step - 1]
            else:
                last_state = rolled_one[:, step]
            if step >= 2:
                older_state = fresh[step - 2]
            else:
                older_state = rolled_two[:, step]
            source = force_slab[:, step] + 2.0 * last_state - 0.5 * older_state
            dens = dens_slab[:, step]
            value = old_slab[:, step]
            for sweep in range(SWEEPS):
                value = mask_float * ((source + dens * neighbours(value)) / (1.5 + 6.0 * dens))
            fresh.append(value)
        pressure = jnp.stack(fresh, axis=1).reshape(forcing.shape)
    dens_all = inv_density.astype(jnp.float32)
    last_all = jnp.roll(pressure, 1, axis=0)
    older_all = jnp.roll(pressure, 2, axis=0)
    residual = mask_float * (forcing - 1.5 * pressure + 2.0 * last_all - 0.5 * older_all
                             - dens_all * (6.0 * pressure - neighbours(pressure)))
    return pressure, residual
```

```python
import functools

import jax
import jax.numpy as jnp
from jax import lax
from jax.experimental import pallas as pl
from jax.experimental.pallas import tpu as pltpu
from jax.sharding import PartitionSpec as P

ITERS = 2
ROWS = 8
PAD = 8


def kernel(
    n_tm, n_space,
    f_hbm, k_hbm, m_hbm, g_hbm, p_out, r_out,
    V, A, B, F, K, M, W, KW, MD, MK, G, R,
    load_sem, out_sem, sa, ra, sb, rb, sh, rh,
):
    planes, height, width = F.shape
    chunks = height // ROWS
    t = lax.axis_index("tm")
    s = lax.axis_index("space")
    even = lax.rem(t, 2) == 0
    odd = lax.rem(t, 2) == 1
    partner = t + 1 - 2 * lax.rem(t, 2)
    ahead = lax.rem(t + 2, n_tm)
    behind = lax.rem(t + n_tm - 2, n_tm)
    has_lo = s > 0
    has_hi = s < n_space - 1

    def rows(c):
        return pl.ds(c * ROWS, ROWS)

    def padded(c):
        return pl.ds(PAD + c * ROWS, ROWS)

    loads = [
        pltpu.make_async_copy(g_hbm.at[0], V.at[0, pl.ds(1, planes), pl.ds(PAD, height)], load_sem.at[0]),
        pltpu.make_async_copy(k_hbm.at[0], K, load_sem.at[1]),
        pltpu.make_async_copy(m_hbm, M, load_sem.at[2]),
        pltpu.make_async_copy(f_hbm.at[0], F, load_sem.at[3]),
    ]
    for load in loads:
        load.start()

    barrier = pltpu.get_barrier_semaphore()
    for other in (partner, ahead, behind):
        pl.semaphore_signal(barrier, inc=1, device_id={"tm": other}, device_id_type=pl.DeviceIdType.MESH)

    @pl.when(has_lo)
    def _():
        pl.semaphore_signal(barrier, inc=1, device_id={"space": s - 1}, device_id_type=pl.DeviceIdType.MESH)

    @pl.when(has_hi)
    def _():
        pl.semaphore_signal(barrier, inc=1, device_id={"space": s + 1}, device_id_type=pl.DeviceIdType.MESH)

    @pl.when(has_lo & has_hi)
    def _():
        pl.semaphore_wait(barrier, 5)

    @pl.when(jnp.logical_not(has_lo & has_hi))
    def _():
        pl.semaphore_wait(barrier, 4)

    def field(e, c):
        if e == 0:
            return g_hbm.at[0, :, rows(c)]
        return V.at[2 * e, pl.ds(1, planes), padded(c)]

    def to_ahead(e, c):
        return pltpu.make_async_remote_copy(
            field(e, c), B.at[e, :, rows(c)], sb.at[e, c], rb.at[e, c],
            device_id={"tm": ahead}, device_id_type=pl.DeviceIdType.MESH)

    def to_partner(e, c):
        return pltpu.make_async_remote_copy(
            field(e, c), A.at[e, :, rows(c)], sa.at[e, c], ra.at[e, c],
            device_id={"tm": partner}, device_id_type=pl.DeviceIdType.MESH)

    def relay(e, c):
        return pltpu.make_async_remote_copy(
            B.at[e, :, rows(c)], A.at[e, :, rows(c)], sa.at[e, c], ra.at[e, c],
            device_id={"tm": partner}, device_id_type=pl.DeviceIdType.MESH)

    def to_lo(i, c):
        src = g_hbm.at[0, 0, rows(c)] if i == 0 else V.at[i, 1, padded(c)]
        return pltpu.make_async_remote_copy(
            src, V.at[i, planes + 1, padded(c)], sh.at[i, 0, c], rh.at[i, 1, c],
            device_id={"space": s - 1}, device_id_type=pl.DeviceIdType.MESH)

    def to_hi(i, c):
        src = g_hbm.at[0, planes - 1, rows(c)] if i == 0 else V.at[i, planes, padded(c)]
        return pltpu.make_async_remote_copy(
            src, V.at[i, 0, padded(c)], sh.at[i, 1, c], rh.at[i, 0, c],
            device_id={"space": s + 1}, device_id_type=pl.DeviceIdType.MESH)

    def send_field(e, c):
        to_ahead(e, c).start()

        @pl.when(even)
        def _():
            to_partner(e, c).start()

    def send_halo(i, c):
        @pl.when(has_lo)
        def _():
            to_lo(i, c).start()

        @pl.when(has_hi)
        def _():
            to_hi(i, c).start()

    def wait_halo(i, c):
        @pl.when(has_lo)
        def _():
            to_hi(i, c).wait_recv()

        @pl.when(has_hi)
        def _():
            to_lo(i, c).wait_recv()

    for c in range(chunks):
        send_field(0, c)
        send_halo(0, c)

    last = 2 * ITERS
    edge = jnp.zeros((PAD, width), jnp.float32)
    for i in range(last + 1):
        def clear(p, _, i=i):
            V[i, p, pl.ds(0, PAD), :] = edge
            V[i, p, pl.ds(PAD + height, PAD), :] = edge
            return 0
        lax.fori_loop(1, planes + 1, clear, 0)

        @pl.when(s == 0)
        def _(i=i):
            V[i, 0, pl.ds(PAD, height), :] = jnp.zeros((height, width), jnp.float32)

        @pl.when(s == n_space - 1)
        def _(i=i):
            V[i, planes + 1, pl.ds(PAD, height), :] = jnp.zeros((height, width), jnp.float32)

    for load in loads:
        load.wait()

    def prepare(p, _):
        for h in range(height // 16):
            at = pl.ds(16 * h, 16)
            k = K[p, at, :].astype(jnp.float32)
            m = M[p, at, :].astype(jnp.float32)
            d = 1.5 + 6.0 * k
            w = m / d
            W[p, at, :] = w
            KW[p, at, :] = k * w
            MD[p, at, :] = m * d
            MK[p, at, :] = m * k
        return 0

    lax.fori_loop(0, planes, prepare, 0)

    lane = lax.broadcasted_iota(jnp.int32, (ROWS, width), 1)

    def beside(i, p, c):
        mid = V[i, p + 1, padded(c), :]
        total = V[i, p, padded(c), :] + V[i, p + 2, padded(c), :]
        total = total + V[i, p + 1, pl.ds(PAD + c * ROWS - 1, ROWS), :]
        total = total + V[i, p + 1, pl.ds(PAD + c * ROWS + 1, ROWS), :]
        total = total + jnp.where(lane == 0, 0.0, pltpu.roll(mid, 1, 1))
        total = total + jnp.where(lane == width - 1, 0.0, pltpu.roll(mid, width - 1, 1))
        return mid, total

    def sweep_first(e, c):
        def step(p, _):
            at = rows(c)
            src = F[p, at, :] + 2.0 * A[e, p, at, :] - 0.5 * B[e, p, at, :]
            g = W[p, at, :] * src
            G[p, at, :] = g
            V[2 * e + 1, p + 1, padded(c), :] = g + KW[p, at, :] * beside(2 * e, p, c)[1]
            return 0
        lax.fori_loop(0, planes, step, 0)

    def sweep_second(e, c):
        def step(p, _):
            at = rows(c)
            V[2 * e + 2, p + 1, padded(c), :] = G[p, at, :] + KW[p, at, :] * beside(2 * e + 1, p, c)[1]
            return 0
        lax.fori_loop(0, planes, step, 0)

    def arrive(e, c):
        to_ahead(e, c).wait_recv()

        @pl.when(odd)
        def _():
            relay(e, c).start()

    def finish(e, c):
        wait_halo(2 * e + 1, c)
        sweep_second(e, c)
        send_field(e + 1, c)
        send_halo(2 * e + 2, c)
        if e == ITERS - 1:
            pltpu.make_async_copy(
                V.at[last, pl.ds(1, planes), padded(c)], p_out.at[0, :, rows(c)], out_sem.at[0, c]
            ).start()

    for e in range(ITERS):
        for c in range(chunks):
            arrive(e, c)
            wait_halo(2 * e, c)
            to_partner(e, c).wait_recv()
            sweep_first(e, c)
            send_halo(2 * e + 1, c)
            if c >= 1:
                finish(e, c - 1)
        finish(e, chunks - 1)

    for c in range(chunks):
        arrive(ITERS, c)
        wait_halo(last, c)

        def partial(p, _, c=c):
            at = rows(c)
            mid, total = beside(last, p, c)
            m = M[p, at, :].astype(jnp.float32)
            R[p, at, :] = m * F[p, at, :] - MD[p, at, :] * mid + MK[p, at, :] * total
            return 0
        lax.fori_loop(0, planes, partial, 0)
        to_partner(ITERS, c).wait_recv()

        def complete(p, _, c=c):
            at = rows(c)
            m = M[p, at, :].astype(jnp.float32)
            R[p, at, :] = R[p, at, :] + m * (2.0 * A[ITERS, p, at, :] - 0.5 * B[ITERS, p, at, :])
            return 0
        lax.fori_loop(0, planes, complete, 0)
        pltpu.make_async_copy(R.at[:, rows(c)], r_out.at[0, :, rows(c)], out_sem.at[1, c]).start()

    for e in range(ITERS + 1):
        for c in range(chunks):
            to_ahead(e, c).wait_send()

            @pl.when(even)
            def _(e=e, c=c):
                to_partner(e, c).wait_send()

            @pl.when(odd)
            def _(e=e, c=c):
                relay(e, c).wait_send()
    for i in range(last + 1):
        for c in range(chunks):
            @pl.when(has_lo)
            def _(i=i, c=c):
                to_lo(i, c).wait_send()

            @pl.when(has_hi)
            def _(i=i, c=c):
                to_hi(i, c).wait_send()
    for c in range(chunks):
        pltpu.make_async_copy(
            V.at[last, pl.ds(1, planes), padded(c)], p_out.at[0, :, rows(c)], out_sem.at[0, c]
        ).wait()
        pltpu.make_async_copy(R.at[:, rows(c)], r_out.at[0, :, rows(c)], out_sem.at[1, c]).wait()


def solution(mesh):
    n_tm, n_space = mesh.shape["tm"], mesh.shape["space"]
    placed = (
        P("tm", "space", None, None),
        P("tm", "space", None, None),
        P("space", None, None),
        P("tm", "space", None, None),
    )

    def body(forcing, inv_density, wall_mask, guess):
        planes, height, width = wall_mask.shape
        chunks = height // ROWS
        full = (planes, height, width)
        exchanges = ITERS + 1
        values = 2 * ITERS + 1
        f32 = jnp.float32
        pressure, residual = pl.pallas_call(
            functools.partial(kernel, n_tm, n_space),
            out_shape=[jax.ShapeDtypeStruct(guess.shape, f32)] * 2,
            in_specs=[pl.BlockSpec(memory_space=pl.ANY)] * 4,
            out_specs=[pl.BlockSpec(memory_space=pl.ANY)] * 2,
            scratch_shapes=[
                pltpu.VMEM((values, planes + 2, height + 2 * PAD, width), f32),
                pltpu.VMEM((exchanges,) + full, f32),
                pltpu.VMEM((exchanges,) + full, f32),
                pltpu.VMEM(full, f32),
                pltpu.VMEM(full, inv_density.dtype),
                pltpu.VMEM(full, wall_mask.dtype),
                pltpu.VMEM(full, f32),
                pltpu.VMEM(full, f32),
                pltpu.VMEM(full, f32),
                pltpu.VMEM(full, f32),
                pltpu.VMEM(full, f32),
                pltpu.VMEM(full, f32),
                pltpu.SemaphoreType.DMA((4,)),
                pltpu.SemaphoreType.DMA((2, chunks)),
                pltpu.SemaphoreType.DMA((exchanges, chunks)),
                pltpu.SemaphoreType.DMA((exchanges, chunks)),
                pltpu.SemaphoreType.DMA((exchanges, chunks)),
                pltpu.SemaphoreType.DMA((exchanges, chunks)),
                pltpu.SemaphoreType.DMA((values, 2, chunks)),
                pltpu.SemaphoreType.DMA((values, 2, chunks)),
            ],
            compiler_params=pltpu.CompilerParams(collective_id=0, has_side_effects=True),
        )(forcing, inv_density, wall_mask, guess)
        return pressure, residual

    return jax.shard_map(
        body,
        mesh=mesh,
        in_specs=placed,
        out_specs=(P("tm", "space", None, None), P("tm", "space", None, None)),
        check_vma=False,
    )
```

```python
import functools

import jax
import jax.numpy as jnp
from jax import lax
from jax.experimental import pallas as pl
from jax.experimental.pallas import tpu as pltpu
from jax.sharding import PartitionSpec as P

ITERS = 2
ROWS = 8
PAD = 8


def kernel(
    n_tm, n_space,
    f_hbm, k_hbm, m_hbm, g_hbm, p_out, r_out,
    V, A, B, F, K, M, W, KW, MD, MK, G, R,
    load_sem, sa, ra, sb, rb, sh, rh,
):
    planes, height, width = F.shape
    chunks = height // ROWS
    t = lax.axis_index("tm")
    s = lax.axis_index("space")
    even = lax.rem(t, 2) == 0
    odd = lax.rem(t, 2) == 1
    partner = t + 1 - 2 * lax.rem(t, 2)
    ahead = lax.rem(t + 2, n_tm)
    behind = lax.rem(t + n_tm - 2, n_tm)
    has_lo = s > 0
    has_hi = s < n_space - 1

    def rows(c):
        return pl.ds(c * ROWS, ROWS)

    def padded(c):
        return pl.ds(PAD + c * ROWS, ROWS)

    loads = [
        pltpu.make_async_copy(g_hbm.at[0], V.at[0, pl.ds(1, planes), pl.ds(PAD, height)], load_sem.at[0]),
        pltpu.make_async_copy(k_hbm.at[0], K, load_sem.at[1]),
        pltpu.make_async_copy(m_hbm, M, load_sem.at[2]),
        pltpu.make_async_copy(f_hbm.at[0], F, load_sem.at[3]),
    ]
    for load in loads:
        load.start()

    barrier = pltpu.get_barrier_semaphore()
    for other in (partner, ahead, behind):
        pl.semaphore_signal(barrier, inc=1, device_id={"tm": other}, device_id_type=pl.DeviceIdType.MESH)

    @pl.when(has_lo)
    def _():
        pl.semaphore_signal(barrier, inc=1, device_id={"space": s - 1}, device_id_type=pl.DeviceIdType.MESH)

    @pl.when(has_hi)
    def _():
        pl.semaphore_signal(barrier, inc=1, device_id={"space": s + 1}, device_id_type=pl.DeviceIdType.MESH)

    @pl.when(has_lo & has_hi)
    def _():
        pl.semaphore_wait(barrier, 5)

    @pl.when(jnp.logical_not(has_lo & has_hi))
    def _():
        pl.semaphore_wait(barrier, 4)

    def field(e, c):
        if e == 0:
            return g_hbm.at[0, :, rows(c)]
        return V.at[2 * e, pl.ds(1, planes), padded(c)]

    def to_ahead(e, c):
        return pltpu.make_async_remote_copy(
            field(e, c), B.at[e, :, rows(c)], sb.at[e, c], rb.at[e, c],
            device_id={"tm": ahead}, device_id_type=pl.DeviceIdType.MESH)

    def to_partner(e, c):
        return pltpu.make_async_remote_copy(
            field(e, c), A.at[e, :, rows(c)], sa.at[e, c], ra.at[e, c],
            device_id={"tm": partner}, device_id_type=pl.DeviceIdType.MESH)

    def relay(e, c):
        return pltpu.make_async_remote_copy(
            B.at[e, :, rows(c)], A.at[e, :, rows(c)], sa.at[e, c], ra.at[e, c],
            device_id={"tm": partner}, device_id_type=pl.DeviceIdType.MESH)

    def to_lo(i, c):
        src = g_hbm.at[0, 0, rows(c)] if i == 0 else V.at[i, 1, padded(c)]
        return pltpu.make_async_remote_copy(
            src, V.at[i, planes + 1, padded(c)], sh.at[i, 0, c], rh.at[i, 1, c],
            device_id={"space": s - 1}, device_id_type=pl.DeviceIdType.MESH)

    def to_hi(i, c):
        src = g_hbm.at[0, planes - 1, rows(c)] if i == 0 else V.at[i, planes, padded(c)]
        return pltpu.make_async_remote_copy(
            src, V.at[i, 0, padded(c)], sh.at[i, 1, c], rh.at[i, 0, c],
            device_id={"space": s + 1}, device_id_type=pl.DeviceIdType.MESH)

    def send_field(e, c):
        to_ahead(e, c).start()

        @pl.when(even)
        def _():
            to_partner(e, c).start()

    def send_halo(i, c):
        @pl.when(has_lo)
        def _():
            to_lo(i, c).start()

        @pl.when(has_hi)
        def _():
            to_hi(i, c).start()

    def wait_halo(i, c):
        @pl.when(has_lo)
        def _():
            to_hi(i, c).wait_recv()

        @pl.when(has_hi)
        def _():
            to_lo(i, c).wait_recv()

    for c in range(chunks):
        send_field(0, c)
        send_halo(0, c)

    last = 2 * ITERS
    edge = jnp.zeros((PAD, width), jnp.float32)
    for i in range(last + 1):
        def clear(p, _, i=i):
            V[i, p, pl.ds(0, PAD), :] = edge
            V[i, p, pl.ds(PAD + height, PAD), :] = edge
            return 0
        lax.fori_loop(1, planes + 1, clear, 0)

        @pl.when(s == 0)
        def _(i=i):
            V[i, 0, pl.ds(PAD, height), :] = jnp.zeros((height, width), jnp.float32)

        @pl.when(s == n_space - 1)
        def _(i=i):
            V[i, planes + 1, pl.ds(PAD, height), :] = jnp.zeros((height, width), jnp.float32)

    for load in loads:
        load.wait()

    def prepare(p, _):
        for h in range(height // 16):
            at = pl.ds(16 * h, 16)
            k = K[p, at, :].astype(jnp.float32)
            m = M[p, at, :].astype(jnp.float32)
            d = 1.5 + 6.0 * k
            w = m / d
            W[p, at, :] = w
            KW[p, at, :] = k * w
            MD[p, at, :] = m * d
            MK[p, at, :] = m * k
        return 0

    lax.fori_loop(0, planes, prepare, 0)

    lane = lax.broadcasted_iota(jnp.int32, (ROWS, width), 1)

    def beside(i, p, c):
        mid = V[i, p + 1, padded(c), :]
        total = V[i, p, padded(c), :] + V[i, p + 2, padded(c), :]
        total = total + V[i, p + 1, pl.ds(PAD + c * ROWS - 1, ROWS), :]
        total = total + V[i, p + 1, pl.ds(PAD + c * ROWS + 1, ROWS), :]
        total = total + jnp.where(lane == 0, 0.0, pltpu.roll(mid, 1, 1))
        total = total + jnp.where(lane == width - 1, 0.0, pltpu.roll(mid, width - 1, 1))
        return mid, total

    def sweep_first(e, c):
        def step(p, _):
            at = rows(c)
            src = F[p, at, :] + 2.0 * A[e, p, at, :] - 0.5 * B[e, p, at, :]
            g = W[p, at, :] * src
            G[p, at, :] = g
            V[2 * e + 1, p + 1, padded(c), :] = g + KW[p, at, :] * beside(2 * e, p, c)[1]
            return 0
        lax.fori_loop(0, planes, step, 0)

    def sweep_second(e, c):
        def step(p, _):
            at = rows(c)
            v = G[p, at, :] + KW[p, at, :] * beside(2 * e + 1, p, c)[1]
            V[2 * e + 2, p + 1, padded(c), :] = v
            if e == ITERS - 1:
                p_out[0, p, at, :] = v
            return 0
        lax.fori_loop(0, planes, step, 0)

    def arrive(e, c):
        to_ahead(e, c).wait_recv()

        @pl.when(odd)
        def _():
            relay(e, c).start()

    def finish(e, c):
        wait_halo(2 * e + 1, c)
        sweep_second(e, c)
        send_field(e + 1, c)
        send_halo(2 * e + 2, c)

    for e in range(ITERS):
        for c in range(chunks):
            arrive(e, c)
            wait_halo(2 * e, c)
            to_partner(e, c).wait_recv()
            sweep_first(e, c)
            send_halo(2 * e + 1, c)
            if c >= 1:
                finish(e, c - 1)
        finish(e, chunks - 1)

    for c in range(chunks):
        arrive(ITERS, c)
        wait_halo(last, c)

        def partial(p, _, c=c):
            at = rows(c)
            mid, total = beside(last, p, c)
            m = M[p, at, :].astype(jnp.float32)
            R[p, at, :] = m * F[p, at, :] - MD[p, at, :] * mid + MK[p, at, :] * total
            return 0
        lax.fori_loop(0, planes, partial, 0)
        to_partner(ITERS, c).wait_recv()

        def complete(p, _, c=c):
            at = rows(c)
            m = M[p, at, :].astype(jnp.float32)
            r_out[0, p, at, :] = R[p, at, :] + m * (2.0 * A[ITERS, p, at, :] - 0.5 * B[ITERS, p, at, :])
            return 0
        lax.fori_loop(0, planes, complete, 0)

    for e in range(ITERS + 1):
        for c in range(chunks):
            to_ahead(e, c).wait_send()

            @pl.when(even)
            def _(e=e, c=c):
                to_partner(e, c).wait_send()

            @pl.when(odd)
            def _(e=e, c=c):
                relay(e, c).wait_send()
    for i in range(last + 1):
        for c in range(chunks):
            @pl.when(has_lo)
            def _(i=i, c=c):
                to_lo(i, c).wait_send()

            @pl.when(has_hi)
            def _(i=i, c=c):
                to_hi(i, c).wait_send()


def solution(mesh):
    n_tm, n_space = mesh.shape["tm"], mesh.shape["space"]
    placed = (
        P("tm", "space", None, None),
        P("tm", "space", None, None),
        P("space", None, None),
        P("tm", "space", None, None),
    )

    def body(forcing, inv_density, wall_mask, guess):
        planes, height, width = wall_mask.shape
        chunks = height // ROWS
        full = (planes, height, width)
        exchanges = ITERS + 1
        values = 2 * ITERS + 1
        f32 = jnp.float32
        pressure, residual = pl.pallas_call(
            functools.partial(kernel, n_tm, n_space),
            out_shape=[pltpu.VMEM(guess.shape, f32)] * 2,
            in_specs=[pl.BlockSpec(memory_space=pl.ANY)] * 4,
            out_specs=[pl.BlockSpec(memory_space=pltpu.VMEM)] * 2,
            scratch_shapes=[
                pltpu.VMEM((values, planes + 2, height + 2 * PAD, width), f32),
                pltpu.VMEM((exchanges,) + full, f32),
                pltpu.VMEM((exchanges,) + full, f32),
                pltpu.VMEM(full, f32),
                pltpu.VMEM(full, inv_density.dtype),
                pltpu.VMEM(full, wall_mask.dtype),
                pltpu.VMEM(full, f32),
                pltpu.VMEM(full, f32),
                pltpu.VMEM(full, f32),
                pltpu.VMEM(full, f32),
                pltpu.VMEM(full, f32),
                pltpu.VMEM(full, f32),
                pltpu.SemaphoreType.DMA((4,)),
                pltpu.SemaphoreType.DMA((exchanges, chunks)),
                pltpu.SemaphoreType.DMA((exchanges, chunks)),
                pltpu.SemaphoreType.DMA((exchanges, chunks)),
                pltpu.SemaphoreType.DMA((exchanges, chunks)),
                pltpu.SemaphoreType.DMA((values, 2, chunks)),
                pltpu.SemaphoreType.DMA((values, 2, chunks)),
            ],
            compiler_params=pltpu.CompilerParams(collective_id=0, has_side_effects=True),
        )(forcing, inv_density, wall_mask, guess)
        return pressure, residual

    return jax.shard_map(
        body,
        mesh=mesh,
        in_specs=placed,
        out_specs=(P("tm", "space", None, None), P("tm", "space", None, None)),
        check_vma=False,
    )
```

```python
import functools

import jax
import jax.numpy as jnp
from jax import lax
from jax.experimental import pallas as pl
from jax.experimental.pallas import tpu as pltpu
from jax.sharding import PartitionSpec as P

ITERS = 2
ROWS = 8
PAD = 8
PARTS = 2


def kernel(
    n_tm, n_space,
    f_hbm, k_hbm, m_hbm, g_hbm, p_out, r_out,
    V, A, B, F, K, M, W, KW, MD, MK, G, R,
    load_sem, sa, ra, sb, rb, sh, rh,
):
    planes, height, width = F.shape
    chunks = height // ROWS
    t = lax.axis_index("tm")
    s = lax.axis_index("space")
    even = lax.rem(t, 2) == 0
    odd = lax.rem(t, 2) == 1
    partner = t + 1 - 2 * lax.rem(t, 2)
    ahead = lax.rem(t + 2, n_tm)
    behind = lax.rem(t + n_tm - 2, n_tm)
    has_lo = s > 0
    has_hi = s < n_space - 1

    def rows(c):
        return pl.ds(c * ROWS, ROWS)

    def padded(c):
        return pl.ds(PAD + c * ROWS, ROWS)

    loads = [
        pltpu.make_async_copy(g_hbm.at[0], V.at[0, pl.ds(1, planes), pl.ds(PAD, height)], load_sem.at[0]),
        pltpu.make_async_copy(k_hbm.at[0], K, load_sem.at[1]),
        pltpu.make_async_copy(m_hbm, M, load_sem.at[2]),
        pltpu.make_async_copy(f_hbm.at[0], F, load_sem.at[3]),
    ]
    for load in loads:
        load.start()

    barrier = pltpu.get_barrier_semaphore()
    for other in (partner, behind):
        pl.semaphore_signal(barrier, inc=1, device_id={"tm": other}, device_id_type=pl.DeviceIdType.MESH)

    @pl.when(has_lo)
    def _():
        pl.semaphore_signal(barrier, inc=1, device_id={"space": s - 1}, device_id_type=pl.DeviceIdType.MESH)

    @pl.when(has_hi)
    def _():
        pl.semaphore_signal(barrier, inc=1, device_id={"space": s + 1}, device_id_type=pl.DeviceIdType.MESH)

    @pl.when(has_lo & has_hi)
    def _():
        pl.semaphore_wait(barrier, 4)

    @pl.when(jnp.logical_not(has_lo & has_hi))
    def _():
        pl.semaphore_wait(barrier, 3)

    share = planes // PARTS

    def part(q):
        return pl.ds(q * share, share)

    def field(e, c, q):
        if e == 0:
            return g_hbm.at[0, part(q), rows(c)]
        return V.at[2 * e, pl.ds(1 + q * share, share), padded(c)]

    def to_ahead(e, c, q):
        return pltpu.make_async_remote_copy(
            field(e, c, q), B.at[e, part(q), rows(c)], sb.at[e, c, q], rb.at[e, c, q],
            device_id={"tm": ahead}, device_id_type=pl.DeviceIdType.MESH)

    def to_partner(e, c, q):
        return pltpu.make_async_remote_copy(
            field(e, c, q), A.at[e, part(q), rows(c)], sa.at[e, c, q], ra.at[e, c, q],
            device_id={"tm": partner}, device_id_type=pl.DeviceIdType.MESH)

    def relay(e, c, q):
        return pltpu.make_async_remote_copy(
            B.at[e, part(q), rows(c)], A.at[e, part(q), rows(c)], sa.at[e, c, q], ra.at[e, c, q],
            device_id={"tm": partner}, device_id_type=pl.DeviceIdType.MESH)

    def to_lo(i, c):
        src = g_hbm.at[0, 0, rows(c)] if i == 0 else V.at[i, 1, padded(c)]
        return pltpu.make_async_remote_copy(
            src, V.at[i, planes + 1, padded(c)], sh.at[i, 0, c], rh.at[i, 1, c],
            device_id={"space": s - 1}, device_id_type=pl.DeviceIdType.MESH)

    def to_hi(i, c):
        src = g_hbm.at[0, planes - 1, rows(c)] if i == 0 else V.at[i, planes, padded(c)]
        return pltpu.make_async_remote_copy(
            src, V.at[i, 0, padded(c)], sh.at[i, 1, c], rh.at[i, 0, c],
            device_id={"space": s + 1}, device_id_type=pl.DeviceIdType.MESH)

    def send_field(e, c):
        for q in range(PARTS):
            to_ahead(e, c, q).start()

        @pl.when(even)
        def _():
            for q in range(PARTS):
                to_partner(e, c, q).start()

    def send_halo(i, c):
        @pl.when(has_lo)
        def _():
            to_lo(i, c).start()

        @pl.when(has_hi)
        def _():
            to_hi(i, c).start()

    def wait_halo(i, c):
        @pl.when(has_lo)
        def _():
            to_hi(i, c).wait_recv()

        @pl.when(has_hi)
        def _():
            to_lo(i, c).wait_recv()

    for c in range(chunks):
        send_field(0, c)
        send_halo(0, c)

    last = 2 * ITERS
    edge = jnp.zeros((PAD, width), jnp.float32)
    for i in range(last + 1):
        def clear(p, _, i=i):
            V[i, p, pl.ds(0, PAD), :] = edge
            V[i, p, pl.ds(PAD + height, PAD), :] = edge
            return 0
        lax.fori_loop(1, planes + 1, clear, 0)

        @pl.when(s == 0)
        def _(i=i):
            V[i, 0, pl.ds(PAD, height), :] = jnp.zeros((height, width), jnp.float32)

        @pl.when(s == n_space - 1)
        def _(i=i):
            V[i, planes + 1, pl.ds(PAD, height), :] = jnp.zeros((height, width), jnp.float32)

    for load in loads:
        load.wait()

    def prepare(p, _):
        for h in range(height // 16):
            at = pl.ds(16 * h, 16)
            k = K[p, at, :].astype(jnp.float32)
            m = M[p, at, :].astype(jnp.float32)
            d = 1.5 + 6.0 * k
            w = m / d
            W[p, at, :] = w
            KW[p, at, :] = k * w
            MD[p, at, :] = m * d
            MK[p, at, :] = m * k
        return 0

    lax.fori_loop(0, planes, prepare, 0)

    lane = lax.broadcasted_iota(jnp.int32, (ROWS, width), 1)

    def beside(i, p, c):
        mid = V[i, p + 1, padded(c), :]
        total = V[i, p, padded(c), :] + V[i, p + 2, padded(c), :]
        total = total + V[i, p + 1, pl.ds(PAD + c * ROWS - 1, ROWS), :]
        total = total + V[i, p + 1, pl.ds(PAD + c * ROWS + 1, ROWS), :]
        total = total + jnp.where(lane == 0, 0.0, pltpu.roll(mid, 1, 1))
        total = total + jnp.where(lane == width - 1, 0.0, pltpu.roll(mid, width - 1, 1))
        return mid, total

    def sweep_first(e, c):
        def step(p, _):
            at = rows(c)
            src = F[p, at, :] + 2.0 * A[e, p, at, :] - 0.5 * B[e, p, at, :]
            g = W[p, at, :] * src
            G[p, at, :] = g
            V[2 * e + 1, p + 1, padded(c), :] = g + KW[p, at, :] * beside(2 * e, p, c)[1]
            return 0
        lax.fori_loop(0, planes, step, 0)

    def sweep_second(e, c):
        def step(p, _):
            at = rows(c)
            v = G[p, at, :] + KW[p, at, :] * beside(2 * e + 1, p, c)[1]
            V[2 * e + 2, p + 1, padded(c), :] = v
            if e == ITERS - 1:
                p_out[0, p, at, :] = v
            return 0
        lax.fori_loop(0, planes, step, 0)

    def arrive(e, c):
        for q in range(PARTS):
            to_ahead(e, c, q).wait_recv()

            @pl.when(odd)
            def _(q=q):
                relay(e, c, q).start()

    def arrive_last(e, c):
        for q in range(PARTS):
            to_partner(e, c, q).wait_recv()

    def finish(e, c):
        wait_halo(2 * e + 1, c)
        sweep_second(e, c)
        send_field(e + 1, c)
        send_halo(2 * e + 2, c)

    for e in range(ITERS):
        for c in range(chunks):
            arrive(e, c)
            wait_halo(2 * e, c)
            arrive_last(e, c)
            sweep_first(e, c)
            send_halo(2 * e + 1, c)
            if c >= 1:
                finish(e, c - 1)
        finish(e, chunks - 1)

    for c in range(chunks):
        arrive(ITERS, c)
        wait_halo(last, c)

        def partial(p, _, c=c):
            at = rows(c)
            mid, total = beside(last, p, c)
            m = M[p, at, :].astype(jnp.float32)
            R[p, at, :] = m * F[p, at, :] - MD[p, at, :] * mid + MK[p, at, :] * total
            return 0
        lax.fori_loop(0, planes, partial, 0)
        arrive_last(ITERS, c)

        def complete(p, _, c=c):
            at = rows(c)
            m = M[p, at, :].astype(jnp.float32)
            r_out[0, p, at, :] = R[p, at, :] + m * (2.0 * A[ITERS, p, at, :] - 0.5 * B[ITERS, p, at, :])
            return 0
        lax.fori_loop(0, planes, complete, 0)

    for e in range(ITERS + 1):
        for c in range(chunks):
            for q in range(PARTS):
                to_ahead(e, c, q).wait_send()

            @pl.when(even)
            def _(e=e, c=c):
                for q in range(PARTS):
                    to_partner(e, c, q).wait_send()

            @pl.when(odd)
            def _(e=e, c=c):
                for q in range(PARTS):
                    relay(e, c, q).wait_send()
    for i in range(last + 1):
        for c in range(chunks):
            @pl.when(has_lo)
            def _(i=i, c=c):
                to_lo(i, c).wait_send()

            @pl.when(has_hi)
            def _(i=i, c=c):
                to_hi(i, c).wait_send()


def solution(mesh):
    n_tm, n_space = mesh.shape["tm"], mesh.shape["space"]
    placed = (
        P("tm", "space", None, None),
        P("tm", "space", None, None),
        P("space", None, None),
        P("tm", "space", None, None),
    )

    def body(forcing, inv_density, wall_mask, guess):
        planes, height, width = wall_mask.shape
        chunks = height // ROWS
        full = (planes, height, width)
        exchanges = ITERS + 1
        values = 2 * ITERS + 1
        f32 = jnp.float32
        pressure, residual = pl.pallas_call(
            functools.partial(kernel, n_tm, n_space),
            out_shape=[pltpu.VMEM(guess.shape, f32)] * 2,
            in_specs=[pl.BlockSpec(memory_space=pl.ANY)] * 4,
            out_specs=[pl.BlockSpec(memory_space=pltpu.VMEM)] * 2,
            scratch_shapes=[
                pltpu.VMEM((values, planes + 2, height + 2 * PAD, width), f32),
                pltpu.VMEM((exchanges,) + full, f32),
                pltpu.VMEM((exchanges,) + full, f32),
                pltpu.VMEM(full, f32),
                pltpu.VMEM(full, inv_density.dtype),
                pltpu.VMEM(full, wall_mask.dtype),
                pltpu.VMEM(full, f32),
                pltpu.VMEM(full, f32),
                pltpu.VMEM(full, f32),
                pltpu.VMEM(full, f32),
                pltpu.VMEM(full, f32),
                pltpu.VMEM(full, f32),
                pltpu.SemaphoreType.DMA((4,)),
                pltpu.SemaphoreType.DMA((exchanges, chunks, PARTS)),
                pltpu.SemaphoreType.DMA((exchanges, chunks, PARTS)),
                pltpu.SemaphoreType.DMA((exchanges, chunks, PARTS)),
                pltpu.SemaphoreType.DMA((exchanges, chunks, PARTS)),
                pltpu.SemaphoreType.DMA((values, 2, chunks)),
                pltpu.SemaphoreType.DMA((values, 2, chunks)),
            ],
            compiler_params=pltpu.CompilerParams(collective_id=0, has_side_effects=True),
        )(forcing, inv_density, wall_mask, guess)
        return pressure, residual

    return jax.shard_map(
        body,
        mesh=mesh,
        in_specs=placed,
        out_specs=(P("tm", "space", None, None), P("tm", "space", None, None)),
        check_vma=False,
    )
```

```python
import functools

import jax
import jax.numpy as jnp
from jax import lax
from jax.experimental import pallas as pl
from jax.experimental.pallas import tpu as pltpu
from jax.sharding import PartitionSpec as P

ITERS = 2
ROWS = 8
PAD = 8
PARTS = 4


def kernel(
    n_tm, n_space,
    f_hbm, k_hbm, m_hbm, g_hbm, p_out, r_out,
    V, A, B, F, K, M, W, KW, MD, MK, G, R,
    load_sem, sa, ra, sb, rb, sh, rh,
):
    planes, height, width = F.shape
    chunks = height // ROWS
    t = lax.axis_index("tm")
    s = lax.axis_index("space")
    even = lax.rem(t, 2) == 0
    odd = lax.rem(t, 2) == 1
    partner = t + 1 - 2 * lax.rem(t, 2)
    ahead = lax.rem(t + 2, n_tm)
    behind = lax.rem(t + n_tm - 2, n_tm)
    has_lo = s > 0
    has_hi = s < n_space - 1

    def rows(c):
        return pl.ds(c * ROWS, ROWS)

    def padded(c):
        return pl.ds(PAD + c * ROWS, ROWS)

    loads = [
        pltpu.make_async_copy(g_hbm.at[0], V.at[0, pl.ds(1, planes), pl.ds(PAD, height)], load_sem.at[0]),
        pltpu.make_async_copy(k_hbm.at[0], K, load_sem.at[1]),
        pltpu.make_async_copy(m_hbm, M, load_sem.at[2]),
        pltpu.make_async_copy(f_hbm.at[0], F, load_sem.at[3]),
    ]
    for load in loads:
        load.start()

    barrier = pltpu.get_barrier_semaphore()
    for other in (partner, behind):
        pl.semaphore_signal(barrier, inc=1, device_id={"tm": other}, device_id_type=pl.DeviceIdType.MESH)

    @pl.when(has_lo)
    def _():
        pl.semaphore_signal(barrier, inc=1, device_id={"space": s - 1}, device_id_type=pl.DeviceIdType.MESH)

    @pl.when(has_hi)
    def _():
        pl.semaphore_signal(barrier, inc=1, device_id={"space": s + 1}, device_id_type=pl.DeviceIdType.MESH)

    @pl.when(has_lo & has_hi)
    def _():
        pl.semaphore_wait(barrier, 4)

    @pl.when(jnp.logical_not(has_lo & has_hi))
    def _():
        pl.semaphore_wait(barrier, 3)

    share = planes // PARTS

    def part(q):
        return pl.ds(q * share, share)

    def field(e, c, q):
        if e == 0:
            return g_hbm.at[0, part(q), rows(c)]
        return V.at[2 * e, pl.ds(1 + q * share, share), padded(c)]

    def to_ahead(e, c, q):
        return pltpu.make_async_remote_copy(
            field(e, c, q), B.at[e, part(q), rows(c)], sb.at[e, c, q], rb.at[e, c, q],
            device_id={"tm": ahead}, device_id_type=pl.DeviceIdType.MESH)

    def to_partner(e, c, q):
        return pltpu.make_async_remote_copy(
            field(e, c, q), A.at[e, part(q), rows(c)], sa.at[e, c, q], ra.at[e, c, q],
            device_id={"tm": partner}, device_id_type=pl.DeviceIdType.MESH)

    def relay(e, c, q):
        return pltpu.make_async_remote_copy(
            B.at[e, part(q), rows(c)], A.at[e, part(q), rows(c)], sa.at[e, c, q], ra.at[e, c, q],
            device_id={"tm": partner}, device_id_type=pl.DeviceIdType.MESH)

    def to_lo(i, c):
        src = g_hbm.at[0, 0, rows(c)] if i == 0 else V.at[i, 1, padded(c)]
        return pltpu.make_async_remote_copy(
            src, V.at[i, planes + 1, padded(c)], sh.at[i, 0, c], rh.at[i, 1, c],
            device_id={"space": s - 1}, device_id_type=pl.DeviceIdType.MESH)

    def to_hi(i, c):
        src = g_hbm.at[0, planes - 1, rows(c)] if i == 0 else V.at[i, planes, padded(c)]
        return pltpu.make_async_remote_copy(
            src, V.at[i, 0, padded(c)], sh.at[i, 1, c], rh.at[i, 0, c],
            device_id={"space": s + 1}, device_id_type=pl.DeviceIdType.MESH)

    def send_field(e, c):
        for q in range(PARTS):
            to_ahead(e, c, q).start()

        @pl.when(even)
        def _():
            for q in range(PARTS):
                to_partner(e, c, q).start()

    def send_halo(i, c):
        @pl.when(has_lo)
        def _():
            to_lo(i, c).start()

        @pl.when(has_hi)
        def _():
            to_hi(i, c).start()

    def wait_halo(i, c):
        @pl.when(has_lo)
        def _():
            to_hi(i, c).wait_recv()

        @pl.when(has_hi)
        def _():
            to_lo(i, c).wait_recv()

    for c in range(chunks):
        send_field(0, c)
        send_halo(0, c)

    last = 2 * ITERS
    edge = jnp.zeros((PAD, width), jnp.float32)
    for i in range(last + 1):
        def clear(p, _, i=i):
            V[i, p, pl.ds(0, PAD), :] = edge
            V[i, p, pl.ds(PAD + height, PAD), :] = edge
            return 0
        lax.fori_loop(1, planes + 1, clear, 0)

        @pl.when(s == 0)
        def _(i=i):
            V[i, 0, pl.ds(PAD, height), :] = jnp.zeros((height, width), jnp.float32)

        @pl.when(s == n_space - 1)
        def _(i=i):
            V[i, planes + 1, pl.ds(PAD, height), :] = jnp.zeros((height, width), jnp.float32)

    for load in loads:
        load.wait()

    def prepare(p, _):
        for h in range(height // 16):
            at = pl.ds(16 * h, 16)
            k = K[p, at, :].astype(jnp.float32)
            m = M[p, at, :].astype(jnp.float32)
            d = 1.5 + 6.0 * k
            w = m / d
            W[p, at, :] = w
            KW[p, at, :] = k * w
            MD[p, at, :] = m * d
            MK[p, at, :] = m * k
        return 0

    lax.fori_loop(0, planes, prepare, 0)

    lane = lax.broadcasted_iota(jnp.int32, (ROWS, width), 1)

    def beside(i, p, c):
        mid = V[i, p + 1, padded(c), :]
        total = V[i, p, padded(c), :] + V[i, p + 2, padded(c), :]
        total = total + V[i, p + 1, pl.ds(PAD + c * ROWS - 1, ROWS), :]
        total = total + V[i, p + 1, pl.ds(PAD + c * ROWS + 1, ROWS), :]
        total = total + jnp.where(lane == 0, 0.0, pltpu.roll(mid, 1, 1))
        total = total + jnp.where(lane == width - 1, 0.0, pltpu.roll(mid, width - 1, 1))
        return mid, total

    def sweep_first(e, c):
        def step(p, _):
            at = rows(c)
            src = F[p, at, :] + 2.0 * A[e, p, at, :] - 0.5 * B[e, p, at, :]
            g = W[p, at, :] * src
            G[p, at, :] = g
            V[2 * e + 1, p + 1, padded(c), :] = g + KW[p, at, :] * beside(2 * e, p, c)[1]
            return 0
        lax.fori_loop(0, planes, step, 0)

    def sweep_second(e, c):
        def step(p, _):
            at = rows(c)
            v = G[p, at, :] + KW[p, at, :] * beside(2 * e + 1, p, c)[1]
            V[2 * e + 2, p + 1, padded(c), :] = v
            if e == ITERS - 1:
                p_out[0, p, at, :] = v
            return 0
        lax.fori_loop(0, planes, step, 0)

    def arrive(e, c):
        for q in range(PARTS):
            to_ahead(e, c, q).wait_recv()

            @pl.when(odd)
            def _(q=q):
                relay(e, c, q).start()

    def arrive_last(e, c):
        for q in range(PARTS):
            to_partner(e, c, q).wait_recv()

    def finish(e, c):
        wait_halo(2 * e + 1, c)
        sweep_second(e, c)
        send_field(e + 1, c)
        send_halo(2 * e + 2, c)

    for e in range(ITERS):
        for c in range(chunks):
            arrive(e, c)
            wait_halo(2 * e, c)
            arrive_last(e, c)
            sweep_first(e, c)
            send_halo(2 * e + 1, c)
            if c >= 1:
                finish(e, c - 1)
        finish(e, chunks - 1)

    for c in range(chunks):
        arrive(ITERS, c)
        wait_halo(last, c)

        def partial(p, _, c=c):
            at = rows(c)
            mid, total = beside(last, p, c)
            m = M[p, at, :].astype(jnp.float32)
            R[p, at, :] = m * F[p, at, :] - MD[p, at, :] * mid + MK[p, at, :] * total
            return 0
        lax.fori_loop(0, planes, partial, 0)
        arrive_last(ITERS, c)

        def complete(p, _, c=c):
            at = rows(c)
            m = M[p, at, :].astype(jnp.float32)
            r_out[0, p, at, :] = R[p, at, :] + m * (2.0 * A[ITERS, p, at, :] - 0.5 * B[ITERS, p, at, :])
            return 0
        lax.fori_loop(0, planes, complete, 0)

    for e in range(ITERS + 1):
        for c in range(chunks):
            for q in range(PARTS):
                to_ahead(e, c, q).wait_send()

            @pl.when(even)
            def _(e=e, c=c):
                for q in range(PARTS):
                    to_partner(e, c, q).wait_send()

            @pl.when(odd)
            def _(e=e, c=c):
                for q in range(PARTS):
                    relay(e, c, q).wait_send()
    for i in range(last + 1):
        for c in range(chunks):
            @pl.when(has_lo)
            def _(i=i, c=c):
                to_lo(i, c).wait_send()

            @pl.when(has_hi)
            def _(i=i, c=c):
                to_hi(i, c).wait_send()


def write_out(p_ref, r_ref, p_out, r_out, sem):
    planes = p_ref.shape[1]
    copies = []
    for i, (src, dst) in enumerate(((p_ref, p_out), (r_ref, r_out))):
        for p in range(planes):
            copies.append(pltpu.make_async_copy(src.at[0, p], dst.at[0, p], sem.at[i, p]))
    for copy in copies:
        copy.start()
    for copy in copies:
        copy.wait()


def solution(mesh):
    n_tm, n_space = mesh.shape["tm"], mesh.shape["space"]
    placed = (
        P("tm", "space", None, None),
        P("tm", "space", None, None),
        P("space", None, None),
        P("tm", "space", None, None),
    )

    def body(forcing, inv_density, wall_mask, guess):
        planes, height, width = wall_mask.shape
        chunks = height // ROWS
        full = (planes, height, width)
        exchanges = ITERS + 1
        values = 2 * ITERS + 1
        f32 = jnp.float32
        pressure, residual = pl.pallas_call(
            functools.partial(kernel, n_tm, n_space),
            out_shape=[pltpu.VMEM(guess.shape, f32)] * 2,
            in_specs=[pl.BlockSpec(memory_space=pl.ANY)] * 4,
            out_specs=[pl.BlockSpec(memory_space=pltpu.VMEM)] * 2,
            scratch_shapes=[
                pltpu.VMEM((values, planes + 2, height + 2 * PAD, width), f32),
                pltpu.VMEM((exchanges,) + full, f32),
                pltpu.VMEM((exchanges,) + full, f32),
                pltpu.VMEM(full, f32),
                pltpu.VMEM(full, inv_density.dtype),
                pltpu.VMEM(full, wall_mask.dtype),
                pltpu.VMEM(full, f32),
                pltpu.VMEM(full, f32),
                pltpu.VMEM(full, f32),
                pltpu.VMEM(full, f32),
                pltpu.VMEM(full, f32),
                pltpu.VMEM(full, f32),
                pltpu.SemaphoreType.DMA((4,)),
                pltpu.SemaphoreType.DMA((exchanges, chunks, PARTS)),
                pltpu.SemaphoreType.DMA((exchanges, chunks, PARTS)),
                pltpu.SemaphoreType.DMA((exchanges, chunks, PARTS)),
                pltpu.SemaphoreType.DMA((exchanges, chunks, PARTS)),
                pltpu.SemaphoreType.DMA((values, 2, chunks)),
                pltpu.SemaphoreType.DMA((values, 2, chunks)),
            ],
            compiler_params=pltpu.CompilerParams(collective_id=0, has_side_effects=True),
        )(forcing, inv_density, wall_mask, guess)
        return pl.pallas_call(
            write_out,
            out_shape=(jax.ShapeDtypeStruct(guess.shape, f32),) * 2,
            in_specs=[pl.BlockSpec(memory_space=pltpu.VMEM)] * 2,
            out_specs=(pl.BlockSpec(memory_space=pl.ANY),) * 2,
            scratch_shapes=[pltpu.SemaphoreType.DMA((2, planes))],
        )(*[pltpu.with_memory_space_constraint(v, pltpu.VMEM) for v in (pressure, residual)])

    return jax.shard_map(
        body,
        mesh=mesh,
        in_specs=placed,
        out_specs=(P("tm", "space", None, None), P("tm", "space", None, None)),
        check_vma=False,
    )
```

```python
import functools

import jax
import jax.numpy as jnp
from jax import lax
from jax.experimental import pallas as pl
from jax.experimental.pallas import tpu as pltpu
from jax.sharding import PartitionSpec as P

ITERS = 2
ROWS = 8
PAD = 8
PARTS = 2


def kernel(
    n_tm, n_space,
    f_hbm, k_hbm, m_hbm, g_hbm, p_out, r_out,
    V, A, B, F, K, M, W, KW, MD, MK, G, R,
    load_sem, sa, ra, sb, rb, sh, rh,
):
    planes, height, width = F.shape
    chunks = height // ROWS
    t = lax.axis_index("tm")
    s = lax.axis_index("space")
    even = lax.rem(t, 2) == 0
    odd = lax.rem(t, 2) == 1
    partner = t + 1 - 2 * lax.rem(t, 2)
    ahead = lax.rem(t + 2, n_tm)
    behind = lax.rem(t + n_tm - 2, n_tm)
    has_lo = s > 0
    has_hi = s < n_space - 1

    def rows(c):
        return pl.ds(c * ROWS, ROWS)

    def padded(c):
        return pl.ds(PAD + c * ROWS, ROWS)

    loads = [
        pltpu.make_async_copy(g_hbm.at[0], V.at[0, pl.ds(1, planes), pl.ds(PAD, height)], load_sem.at[0]),
        pltpu.make_async_copy(k_hbm.at[0], K, load_sem.at[1]),
        pltpu.make_async_copy(m_hbm, M, load_sem.at[2]),
        pltpu.make_async_copy(f_hbm.at[0], F, load_sem.at[3]),
    ]
    for load in loads:
        load.start()

    barrier = pltpu.get_barrier_semaphore()
    for other in (partner, behind):
        pl.semaphore_signal(barrier, inc=1, device_id={"tm": other}, device_id_type=pl.DeviceIdType.MESH)

    @pl.when(has_lo)
    def _():
        pl.semaphore_signal(barrier, inc=1, device_id={"space": s - 1}, device_id_type=pl.DeviceIdType.MESH)

    @pl.when(has_hi)
    def _():
        pl.semaphore_signal(barrier, inc=1, device_id={"space": s + 1}, device_id_type=pl.DeviceIdType.MESH)

    @pl.when(has_lo & has_hi)
    def _():
        pl.semaphore_wait(barrier, 4)

    @pl.when(jnp.logical_not(has_lo & has_hi))
    def _():
        pl.semaphore_wait(barrier, 3)

    share = planes // PARTS

    def part(q):
        return pl.ds(q * share, share)

    def field(e, c, q):
        if e == 0:
            return g_hbm.at[0, part(q), rows(c)]
        return V.at[2 * e, pl.ds(1 + q * share, share), padded(c)]

    def to_ahead(e, c, q):
        return pltpu.make_async_remote_copy(
            field(e, c, q), B.at[e, part(q), rows(c)], sb.at[e, c, q], rb.at[e, c, q],
            device_id={"tm": ahead}, device_id_type=pl.DeviceIdType.MESH)

    def to_partner(e, c, q):
        return pltpu.make_async_remote_copy(
            field(e, c, q), A.at[e, part(q), rows(c)], sa.at[e, c, q], ra.at[e, c, q],
            device_id={"tm": partner}, device_id_type=pl.DeviceIdType.MESH)

    def relay(e, c, q):
        return pltpu.make_async_remote_copy(
            B.at[e, part(q), rows(c)], A.at[e, part(q), rows(c)], sa.at[e, c, q], ra.at[e, c, q],
            device_id={"tm": partner}, device_id_type=pl.DeviceIdType.MESH)

    def to_lo(i, c):
        src = g_hbm.at[0, 0, rows(c)] if i == 0 else V.at[i, 1, padded(c)]
        return pltpu.make_async_remote_copy(
            src, V.at[i, planes + 1, padded(c)], sh.at[i, 0, c], rh.at[i, 1, c],
            device_id={"space": s - 1}, device_id_type=pl.DeviceIdType.MESH)

    def to_hi(i, c):
        src = g_hbm.at[0, planes - 1, rows(c)] if i == 0 else V.at[i, planes, padded(c)]
        return pltpu.make_async_remote_copy(
            src, V.at[i, 0, padded(c)], sh.at[i, 1, c], rh.at[i, 0, c],
            device_id={"space": s + 1}, device_id_type=pl.DeviceIdType.MESH)

    def send_field(e, c):
        for q in range(PARTS):
            to_ahead(e, c, q).start()

        @pl.when(even)
        def _():
            for q in range(PARTS):
                to_partner(e, c, q).start()

    def send_halo(i, c):
        @pl.when(has_lo)
        def _():
            to_lo(i, c).start()

        @pl.when(has_hi)
        def _():
            to_hi(i, c).start()

    def wait_halo(i, c):
        @pl.when(has_lo)
        def _():
            to_hi(i, c).wait_recv()

        @pl.when(has_hi)
        def _():
            to_lo(i, c).wait_recv()

    for c in range(chunks):
        send_field(0, c)
        send_halo(0, c)

    last = 2 * ITERS
    edge = jnp.zeros((PAD, width), jnp.float32)
    for i in range(last + 1):
        def clear(p, _, i=i):
            V[i, p, pl.ds(0, PAD), :] = edge
            V[i, p, pl.ds(PAD + height, PAD), :] = edge
            return 0
        lax.fori_loop(1, planes + 1, clear, 0)

        @pl.when(s == 0)
        def _(i=i):
            V[i, 0, pl.ds(PAD, height), :] = jnp.zeros((height, width), jnp.float32)

        @pl.when(s == n_space - 1)
        def _(i=i):
            V[i, planes + 1, pl.ds(PAD, height), :] = jnp.zeros((height, width), jnp.float32)

    for load in loads:
        load.wait()

    def prepare(p, _):
        for h in range(height // 16):
            at = pl.ds(16 * h, 16)
            k = K[p, at, :].astype(jnp.float32)
            m = M[p, at, :].astype(jnp.float32)
            d = 1.5 + 6.0 * k
            w = m / d
            W[p, at, :] = w
            KW[p, at, :] = k * w
            MD[p, at, :] = m * d
            MK[p, at, :] = m * k
        return 0

    lax.fori_loop(0, planes, prepare, 0)

    lane = lax.broadcasted_iota(jnp.int32, (ROWS, width), 1)

    def beside(i, p, c):
        mid = V[i, p + 1, padded(c), :]
        total = V[i, p, padded(c), :] + V[i, p + 2, padded(c), :]
        total = total + V[i, p + 1, pl.ds(PAD + c * ROWS - 1, ROWS), :]
        total = total + V[i, p + 1, pl.ds(PAD + c * ROWS + 1, ROWS), :]
        total = total + jnp.where(lane == 0, 0.0, pltpu.roll(mid, 1, 1))
        total = total + jnp.where(lane == width - 1, 0.0, pltpu.roll(mid, width - 1, 1))
        return mid, total

    def sweep_first(e, c):
        def step(p, _):
            at = rows(c)
            src = F[p, at, :] + 2.0 * A[e, p, at, :] - 0.5 * B[e, p, at, :]
            g = W[p, at, :] * src
            G[p, at, :] = g
            V[2 * e + 1, p + 1, padded(c), :] = g + KW[p, at, :] * beside(2 * e, p, c)[1]
            return 0
        lax.fori_loop(0, planes, step, 0)

    def sweep_second(e, c):
        def step(p, _):
            at = rows(c)
            v = G[p, at, :] + KW[p, at, :] * beside(2 * e + 1, p, c)[1]
            V[2 * e + 2, p + 1, padded(c), :] = v
            if e == ITERS - 1:
                p_out[0, p, at, :] = v
            return 0
        lax.fori_loop(0, planes, step, 0)

    def arrive(e, c):
        for q in range(PARTS):
            to_ahead(e, c, q).wait_recv()

            @pl.when(odd)
            def _(q=q):
                relay(e, c, q).start()

    def arrive_last(e, c):
        for q in range(PARTS):
            to_partner(e, c, q).wait_recv()

    def finish(e, c):
        wait_halo(2 * e + 1, c)
        sweep_second(e, c)
        send_field(e + 1, c)
        send_halo(2 * e + 2, c)

    for e in range(ITERS):
        for c in range(chunks):
            arrive(e, c)
            wait_halo(2 * e, c)
            arrive_last(e, c)
            sweep_first(e, c)
            send_halo(2 * e + 1, c)
            if c >= 1:
                finish(e, c - 1)
        finish(e, chunks - 1)

    for c in range(chunks):
        arrive(ITERS, c)
        wait_halo(last, c)

        def partial(p, _, c=c):
            at = rows(c)
            mid, total = beside(last, p, c)
            m = M[p, at, :].astype(jnp.float32)
            R[p, at, :] = m * F[p, at, :] - MD[p, at, :] * mid + MK[p, at, :] * total
            return 0
        lax.fori_loop(0, planes, partial, 0)
        arrive_last(ITERS, c)

        def complete(p, _, c=c):
            at = rows(c)
            m = M[p, at, :].astype(jnp.float32)
            r_out[0, p, at, :] = R[p, at, :] + m * (2.0 * A[ITERS, p, at, :] - 0.5 * B[ITERS, p, at, :])
            return 0
        lax.fori_loop(0, planes, complete, 0)

    for e in range(ITERS + 1):
        for c in range(chunks):
            for q in range(PARTS):
                to_ahead(e, c, q).wait_send()

            @pl.when(even)
            def _(e=e, c=c):
                for q in range(PARTS):
                    to_partner(e, c, q).wait_send()

            @pl.when(odd)
            def _(e=e, c=c):
                for q in range(PARTS):
                    relay(e, c, q).wait_send()
    for i in range(last + 1):
        for c in range(chunks):
            @pl.when(has_lo)
            def _(i=i, c=c):
                to_lo(i, c).wait_send()

            @pl.when(has_hi)
            def _(i=i, c=c):
                to_hi(i, c).wait_send()


def write_out(p_ref, r_ref, p_out, r_out, sem):
    planes = p_ref.shape[1]
    copies = []
    for i, (src, dst) in enumerate(((p_ref, p_out), (r_ref, r_out))):
        for p in range(planes):
            copies.append(pltpu.make_async_copy(src.at[0, p], dst.at[0, p], sem.at[i, p]))
    for copy in copies:
        copy.start()
    for copy in copies:
        copy.wait()


def solution(mesh):
    n_tm, n_space = mesh.shape["tm"], mesh.shape["space"]
    placed = (
        P("tm", "space", None, None),
        P("tm", "space", None, None),
        P("space", None, None),
        P("tm", "space", None, None),
    )

    def body(forcing, inv_density, wall_mask, guess):
        planes, height, width = wall_mask.shape
        chunks = height // ROWS
        full = (planes, height, width)
        exchanges = ITERS + 1
        values = 2 * ITERS + 1
        f32 = jnp.float32
        pressure, residual = pl.pallas_call(
            functools.partial(kernel, n_tm, n_space),
            out_shape=[pltpu.VMEM(guess.shape, f32)] * 2,
            in_specs=[pl.BlockSpec(memory_space=pl.ANY)] * 4,
            out_specs=[pl.BlockSpec(memory_space=pltpu.VMEM)] * 2,
            scratch_shapes=[
                pltpu.VMEM((values, planes + 2, height + 2 * PAD, width), f32),
                pltpu.VMEM((exchanges,) + full, f32),
                pltpu.VMEM((exchanges,) + full, f32),
                pltpu.VMEM(full, f32),
                pltpu.VMEM(full, inv_density.dtype),
                pltpu.VMEM(full, wall_mask.dtype),
                pltpu.VMEM(full, f32),
                pltpu.VMEM(full, f32),
                pltpu.VMEM(full, f32),
                pltpu.VMEM(full, f32),
                pltpu.VMEM(full, f32),
                pltpu.VMEM(full, f32),
                pltpu.SemaphoreType.DMA((4,)),
                pltpu.SemaphoreType.DMA((exchanges, chunks, PARTS)),
                pltpu.SemaphoreType.DMA((exchanges, chunks, PARTS)),
                pltpu.SemaphoreType.DMA((exchanges, chunks, PARTS)),
                pltpu.SemaphoreType.DMA((exchanges, chunks, PARTS)),
                pltpu.SemaphoreType.DMA((values, 2, chunks)),
                pltpu.SemaphoreType.DMA((values, 2, chunks)),
            ],
            compiler_params=pltpu.CompilerParams(collective_id=0, has_side_effects=True),
        )(forcing, inv_density, wall_mask, guess)
        return pl.pallas_call(
            write_out,
            out_shape=(jax.ShapeDtypeStruct(guess.shape, f32),) * 2,
            in_specs=[pl.BlockSpec(memory_space=pltpu.VMEM)] * 2,
            out_specs=(pl.BlockSpec(memory_space=pl.ANY),) * 2,
            scratch_shapes=[pltpu.SemaphoreType.DMA((2, planes))],
        )(*[pltpu.with_memory_space_constraint(v, pltpu.VMEM) for v in (pressure, residual)])

    return jax.shard_map(
        body,
        mesh=mesh,
        in_specs=placed,
        out_specs=(P("tm", "space", None, None), P("tm", "space", None, None)),
        check_vma=False,
    )
```

```python
import functools

import jax
import jax.numpy as jnp
from jax import lax
from jax.experimental import pallas as pl
from jax.experimental.pallas import tpu as pltpu
from jax.sharding import PartitionSpec as P

ITERS = 2
ROWS = 8
PAD = 8
PARTS = 2


def kernel(
    n_tm, n_space,
    f_hbm, k_hbm, m_hbm, g_hbm, p_out, r_out,
    V, A, B, F, K, M, W, KW, MD, MK, G, R,
    load_sem, sa, ra, sb, rb, sh, rh,
):
    planes, height, width = F.shape
    chunks = height // ROWS
    t = lax.axis_index("tm")
    s = lax.axis_index("space")
    even = lax.rem(t, 2) == 0
    odd = lax.rem(t, 2) == 1
    partner = t + 1 - 2 * lax.rem(t, 2)
    ahead = lax.rem(t + 2, n_tm)
    behind = lax.rem(t + n_tm - 2, n_tm)
    has_lo = s > 0
    has_hi = s < n_space - 1

    def rows(c):
        return pl.ds(c * ROWS, ROWS)

    def padded(c):
        return pl.ds(PAD + c * ROWS, ROWS)

    loads = [
        pltpu.make_async_copy(g_hbm.at[0], V.at[0, pl.ds(1, planes), pl.ds(PAD, height)], load_sem.at[0]),
        pltpu.make_async_copy(k_hbm.at[0], K, load_sem.at[1]),
        pltpu.make_async_copy(m_hbm, M, load_sem.at[2]),
        pltpu.make_async_copy(f_hbm.at[0], F, load_sem.at[3]),
    ]
    barrier = pltpu.get_barrier_semaphore()
    for other in (partner, behind):
        pl.semaphore_signal(barrier, inc=1, device_id={"tm": other}, device_id_type=pl.DeviceIdType.MESH)

    @pl.when(has_lo)
    def _():
        pl.semaphore_signal(barrier, inc=1, device_id={"space": s - 1}, device_id_type=pl.DeviceIdType.MESH)

    @pl.when(has_hi)
    def _():
        pl.semaphore_signal(barrier, inc=1, device_id={"space": s + 1}, device_id_type=pl.DeviceIdType.MESH)

    for load in loads:
        load.start()

    @pl.when(has_lo & has_hi)
    def _():
        pl.semaphore_wait(barrier, 4)

    @pl.when(jnp.logical_not(has_lo & has_hi))
    def _():
        pl.semaphore_wait(barrier, 3)

    share = planes // PARTS

    def part(q):
        return pl.ds(q * share, share)

    def field(e, c, q):
        if e == 0:
            return g_hbm.at[0, part(q), rows(c)]
        return V.at[2 * e, pl.ds(1 + q * share, share), padded(c)]

    def to_ahead(e, c, q):
        return pltpu.make_async_remote_copy(
            field(e, c, q), B.at[e, part(q), rows(c)], sb.at[e, c, q], rb.at[e, c, q],
            device_id={"tm": ahead}, device_id_type=pl.DeviceIdType.MESH)

    def to_partner(e, c, q):
        return pltpu.make_async_remote_copy(
            field(e, c, q), A.at[e, part(q), rows(c)], sa.at[e, c, q], ra.at[e, c, q],
            device_id={"tm": partner}, device_id_type=pl.DeviceIdType.MESH)

    def relay(e, c, q):
        return pltpu.make_async_remote_copy(
            B.at[e, part(q), rows(c)], A.at[e, part(q), rows(c)], sa.at[e, c, q], ra.at[e, c, q],
            device_id={"tm": partner}, device_id_type=pl.DeviceIdType.MESH)

    def to_lo(i, c):
        src = g_hbm.at[0, 0, rows(c)] if i == 0 else V.at[i, 1, padded(c)]
        return pltpu.make_async_remote_copy(
            src, V.at[i, planes + 1, padded(c)], sh.at[i, 0, c], rh.at[i, 1, c],
            device_id={"space": s - 1}, device_id_type=pl.DeviceIdType.MESH)

    def to_hi(i, c):
        src = g_hbm.at[0, planes - 1, rows(c)] if i == 0 else V.at[i, planes, padded(c)]
        return pltpu.make_async_remote_copy(
            src, V.at[i, 0, padded(c)], sh.at[i, 1, c], rh.at[i, 0, c],
            device_id={"space": s + 1}, device_id_type=pl.DeviceIdType.MESH)

    def send_field(e, c):
        for q in range(PARTS):
            to_ahead(e, c, q).start()

        @pl.when(even)
        def _():
            for q in range(PARTS):
                to_partner(e, c, q).start()

    def send_halo(i, c):
        @pl.when(has_lo)
        def _():
            to_lo(i, c).start()

        @pl.when(has_hi)
        def _():
            to_hi(i, c).start()

    def wait_halo(i, c):
        @pl.when(has_lo)
        def _():
            to_hi(i, c).wait_recv()

        @pl.when(has_hi)
        def _():
            to_lo(i, c).wait_recv()

    for c in range(chunks):
        send_field(0, c)
        send_halo(0, c)

    last = 2 * ITERS
    edge = jnp.zeros((PAD, width), jnp.float32)
    for i in range(last + 1):
        def clear(p, _, i=i):
            V[i, p, pl.ds(0, PAD), :] = edge
            V[i, p, pl.ds(PAD + height, PAD), :] = edge
            return 0
        lax.fori_loop(1, planes + 1, clear, 0)

        @pl.when(s == 0)
        def _(i=i):
            V[i, 0, pl.ds(PAD, height), :] = jnp.zeros((height, width), jnp.float32)

        @pl.when(s == n_space - 1)
        def _(i=i):
            V[i, planes + 1, pl.ds(PAD, height), :] = jnp.zeros((height, width), jnp.float32)

    for load in loads:
        load.wait()

    def prepare(p, _):
        for h in range(height // 16):
            at = pl.ds(16 * h, 16)
            k = K[p, at, :].astype(jnp.float32)
            m = M[p, at, :].astype(jnp.float32)
            d = 1.5 + 6.0 * k
            w = m / d
            W[p, at, :] = w
            KW[p, at, :] = k * w
            MD[p, at, :] = m * d
            MK[p, at, :] = m * k
        return 0

    lax.fori_loop(0, planes, prepare, 0)

    lane = lax.broadcasted_iota(jnp.int32, (ROWS, width), 1)

    def beside(i, p, c):
        mid = V[i, p + 1, padded(c), :]
        total = V[i, p, padded(c), :] + V[i, p + 2, padded(c), :]
        total = total + V[i, p + 1, pl.ds(PAD + c * ROWS - 1, ROWS), :]
        total = total + V[i, p + 1, pl.ds(PAD + c * ROWS + 1, ROWS), :]
        total = total + jnp.where(lane == 0, 0.0, pltpu.roll(mid, 1, 1))
        total = total + jnp.where(lane == width - 1, 0.0, pltpu.roll(mid, width - 1, 1))
        return mid, total

    def sweep_first(e, c):
        def step(p, _):
            at = rows(c)
            src = F[p, at, :] + 2.0 * A[e, p, at, :] - 0.5 * B[e, p, at, :]
            g = W[p, at, :] * src
            G[p, at, :] = g
            V[2 * e + 1, p + 1, padded(c), :] = g + KW[p, at, :] * beside(2 * e, p, c)[1]
            return 0
        lax.fori_loop(0, planes, step, 0)

    def sweep_second(e, c):
        def step(p, _):
            at = rows(c)
            v = G[p, at, :] + KW[p, at, :] * beside(2 * e + 1, p, c)[1]
            V[2 * e + 2, p + 1, padded(c), :] = v
            if e == ITERS - 1:
                p_out[0, p, at, :] = v
            return 0
        lax.fori_loop(0, planes, step, 0)

    def arrive(e, c):
        for q in range(PARTS):
            to_ahead(e, c, q).wait_recv()

            @pl.when(odd)
            def _(q=q):
                relay(e, c, q).start()

    def arrive_last(e, c):
        for q in range(PARTS):
            to_partner(e, c, q).wait_recv()

    def finish(e, c):
        wait_halo(2 * e + 1, c)
        sweep_second(e, c)
        send_field(e + 1, c)
        send_halo(2 * e + 2, c)

    for e in range(ITERS):
        for c in range(chunks):
            arrive(e, c)
            wait_halo(2 * e, c)
            arrive_last(e, c)
            sweep_first(e, c)
            send_halo(2 * e + 1, c)
            if c >= 1:
                finish(e, c - 1)
        finish(e, chunks - 1)

    for c in range(chunks):
        arrive(ITERS, c)
        wait_halo(last, c)

        def partial(p, _, c=c):
            at = rows(c)
            mid, total = beside(last, p, c)
            m = M[p, at, :].astype(jnp.float32)
            R[p, at, :] = m * F[p, at, :] - MD[p, at, :] * mid + MK[p, at, :] * total
            return 0
        lax.fori_loop(0, planes, partial, 0)
        arrive_last(ITERS, c)

        def complete(p, _, c=c):
            at = rows(c)
            m = M[p, at, :].astype(jnp.float32)
            r_out[0, p, at, :] = R[p, at, :] + m * (2.0 * A[ITERS, p, at, :] - 0.5 * B[ITERS, p, at, :])
            return 0
        lax.fori_loop(0, planes, complete, 0)

    for e in range(ITERS + 1):
        for c in range(chunks):
            for q in range(PARTS):
                to_ahead(e, c, q).wait_send()

            @pl.when(even)
            def _(e=e, c=c):
                for q in range(PARTS):
                    to_partner(e, c, q).wait_send()

            @pl.when(odd)
            def _(e=e, c=c):
                for q in range(PARTS):
                    relay(e, c, q).wait_send()
    for i in range(last + 1):
        for c in range(chunks):
            @pl.when(has_lo)
            def _(i=i, c=c):
                to_lo(i, c).wait_send()

            @pl.when(has_hi)
            def _(i=i, c=c):
                to_hi(i, c).wait_send()


def write_out(p_ref, r_ref, p_out, r_out, sem):
    planes = p_ref.shape[1]
    copies = []
    for i, (src, dst) in enumerate(((p_ref, p_out), (r_ref, r_out))):
        for p in range(planes):
            copies.append(pltpu.make_async_copy(src.at[0, p], dst.at[0, p], sem.at[i, p]))
    for copy in copies:
        copy.start()
    for copy in copies:
        copy.wait()


def solution(mesh):
    n_tm, n_space = mesh.shape["tm"], mesh.shape["space"]
    placed = (
        P("tm", "space", None, None),
        P("tm", "space", None, None),
        P("space", None, None),
        P("tm", "space", None, None),
    )

    def body(forcing, inv_density, wall_mask, guess):
        planes, height, width = wall_mask.shape
        chunks = height // ROWS
        full = (planes, height, width)
        exchanges = ITERS + 1
        values = 2 * ITERS + 1
        f32 = jnp.float32
        pressure, residual = pl.pallas_call(
            functools.partial(kernel, n_tm, n_space),
            out_shape=[pltpu.VMEM(guess.shape, f32)] * 2,
            in_specs=[pl.BlockSpec(memory_space=pl.ANY)] * 4,
            out_specs=[pl.BlockSpec(memory_space=pltpu.VMEM)] * 2,
            scratch_shapes=[
                pltpu.VMEM((values, planes + 2, height + 2 * PAD, width), f32),
                pltpu.VMEM((exchanges,) + full, f32),
                pltpu.VMEM((exchanges,) + full, f32),
                pltpu.VMEM(full, f32),
                pltpu.VMEM(full, inv_density.dtype),
                pltpu.VMEM(full, wall_mask.dtype),
                pltpu.VMEM(full, f32),
                pltpu.VMEM(full, f32),
                pltpu.VMEM(full, f32),
                pltpu.VMEM(full, f32),
                pltpu.VMEM(full, f32),
                pltpu.VMEM(full, f32),
                pltpu.SemaphoreType.DMA((4,)),
                pltpu.SemaphoreType.DMA((exchanges, chunks, PARTS)),
                pltpu.SemaphoreType.DMA((exchanges, chunks, PARTS)),
                pltpu.SemaphoreType.DMA((exchanges, chunks, PARTS)),
                pltpu.SemaphoreType.DMA((exchanges, chunks, PARTS)),
                pltpu.SemaphoreType.DMA((values, 2, chunks)),
                pltpu.SemaphoreType.DMA((values, 2, chunks)),
            ],
            compiler_params=pltpu.CompilerParams(collective_id=0, has_side_effects=True),
        )(forcing, inv_density, wall_mask, guess)
        return pl.pallas_call(
            write_out,
            out_shape=(jax.ShapeDtypeStruct(guess.shape, f32),) * 2,
            in_specs=[pl.BlockSpec(memory_space=pltpu.VMEM)] * 2,
            out_specs=(pl.BlockSpec(memory_space=pl.ANY),) * 2,
            scratch_shapes=[pltpu.SemaphoreType.DMA((2, planes))],
        )(*[pltpu.with_memory_space_constraint(v, pltpu.VMEM) for v in (pressure, residual)])

    return jax.shard_map(
        body,
        mesh=mesh,
        in_specs=placed,
        out_specs=(P("tm", "space", None, None), P("tm", "space", None, None)),
        check_vma=False,
    )
```
